256 devices in a mesh: box: 64 (over y, x, z_lo, core), dir: 4 (over z_hi).
Axes of the slice: x: 4, y: 4, z: 8 (z_hi: 4, z_lo: 2; z = z_hi * 2 + z_lo), core: 2. Of those that a mesh axis runs over, the one named last changes fastest.
Arguments:
- child_field: float32 [2, 4, 2048, 4608], P(None, None, 'box', 'dir'), may hold values from -6 to 6
- child_of: int32 [512, 4], P('box'), may hold values from 0 to 2047, as said below
- shift_angle: float32 [4, 18432], P(None, 'dir'), may hold values from -3.140625 to 3.140625
- interp_index: int32 [6, 18432], P(None, 'dir'), may hold values from 0 to 4607, as said below
- interp_weight: float32 [6, 18432], P(None, 'dir'), may hold values from -0.2 to 0.5
- interaction_list: int32 [27, 512], replicated, may hold values from 0 to 511
- translation: float32 [2, 27, 18432], P(None, None, 'dir'), may hold values from -0.875 to 0.875
Outputs:
- child_incoming: float32 [2, 4, 2048, 4608], P(None, None, 'box', 'dir')
The draws below stay inside these ranges and needn't reach their ends.
Inputs may be any that keep to these rules, and one draw needn't show every extreme that they name: child_of lists every child box once; the parents p with p // 8 = q have exactly the children q * 32 to (q + 1) * 32 - 1. interp_index[j, k] differs from k // 4 by at most 8, and for j = 0 by exactly 8 where k // 4 lies 8 or more from both ends.
All inputs are finite; a program needn't handle non-finite values.
Results may differ from the reference program's by a relative error of at most 0.00007.
Values sent between devices are 32-bit elements; how exact they have to be, the bound alone decides.
No kernel may reach another device: no remote copies, remote signals or barrier semaphores. Data moves between devices by JAX's collectives and lax.ppermute only.
A program may use at most 64 MiB of HBM per device.

```python
import math
import jax
import jax.numpy as jnp
from jax import lax

K1 = 4608
K2 = 18432
RHS = 4
KIDS = 4
LIST = 27
STENCIL = 6
HW = 8
BOX_DEV = 32
NB = 2048
NP = 512


def draw_child_of(key, part):
    group_count = NB // BOX_DEV
    keys = jax.random.split(jax.random.fold_in(key, 11), group_count)
    orders = jax.vmap(lambda single: jax.random.permutation(single, BOX_DEV))(keys)
    orders = orders + jnp.arange(group_count, dtype=jnp.int32)[:, None] * BOX_DEV
    return orders.reshape(NP, KIDS).astype(jnp.int32)


def draw_interp_index(key, part):
    offsets = jax.random.randint(jax.random.fold_in(key, 23), (STENCIL, K2), -HW, HW + 1)
    centres = jnp.arange(K2, dtype=jnp.int32)
    edges = jnp.where(centres % 2 == 0, -HW, HW).astype(jnp.int32)
    offsets = offsets.at[0].set(edges)
    return jnp.clip(centres // 4 + offsets, 0, K1 - 1).astype(jnp.int32)


def plant(drawn, rng, low, top_value):
    shape = drawn.shape
    place = [jax.random.randint(jax.random.fold_in(rng, axis), (), 0, shape[axis]) for axis in range(len(shape))]
    drawn = drawn.at[tuple(place)].set(low)
    longest = shape.index(max(shape))
    place[longest] = (place[longest] + 1) % shape[longest]
    return drawn.at[tuple(place)].set(top_value)


def level_of(key, extent, cuts, smallest, largest):
    factor_of = 1.0
    for axis_at, parts in cuts:
        draws = jax.random.uniform(jax.random.fold_in(jax.random.fold_in(key, 6), axis_at), (parts,), jnp.float32, smallest / len(cuts), largest / len(cuts))
        factor_of = factor_of * jnp.repeat(jnp.exp(draws), extent[axis_at] // parts).reshape((-1,) + (1,) * (len(extent) - 1 - axis_at))
    return factor_of


def bell_draw(own_key, extent, scale, reach, shards=(), kind=jnp.bfloat16):
    drawn = jax.random.normal(own_key, extent, jnp.float32) * scale
    if len(shards) > 0:
        drawn = level_of(own_key, extent, shards, -0.22, 0.18) * drawn
    return jnp.clip(drawn, min=-reach, max=reach).astype(kind)


def setup_inputs(seed: int = 0) -> dict:
    splits = jax.random.split(jax.random.key(seed), 8)
    return {
        "child_field": bell_draw(splits[0], (2, RHS, NB, K1), 1.0, 6.0, ((2, 64), (3, 4)), jnp.float32),
        "child_of": draw_child_of(jax.random.fold_in(splits[7], 71), 0),
        "shift_angle": jnp.clip(jax.random.uniform(splits[2], (KIDS, K2), jnp.float32, -3.140625, 3.140625), -3.140625, 3.140625),
        "interp_index": draw_interp_index(jax.random.fold_in(splits[7], 71), 0),
        "interp_weight": jnp.clip(-0.2 + 0.7 * jax.random.uniform(splits[4], (STENCIL, K2), jnp.float32) ** level_of(splits[4], (STENCIL, K2), ((1, 4),), -0.2, 0.2), -0.2, 0.5),
        "interaction_list": plant(jax.random.randint(splits[5], (LIST, NP), 0, NP), jax.random.fold_in(splits[5], 1), 0, NP - 1).astype(jnp.int32),
        "translation": bell_draw(splits[6], (2, LIST, K2), (2 * LIST) ** -0.5, 0.875, ((2, 4),), jnp.float32),
    }


def interpolate(values, index_table, weight_table):
    summed = jnp.zeros(values.shape[:-1] + (index_table.shape[1],), jnp.float32)
    for column in range(index_table.shape[0]):
        summed = summed + weight_table[column] * jnp.take(values, index_table[column], axis=-1)
    return summed


def anterpolate(values, index_table, weight_table):
    summed = jnp.zeros(values.shape[:-1] + (K1,), jnp.float32)
    for column in range(index_table.shape[0]):
        summed = summed.at[..., index_table[column]].add(weight_table[column] * values)
    return summed


def reference(child_field, child_of, shift_angle, interp_index, interp_weight, interaction_list, translation):
    cosines = jnp.cos(shift_angle)
    sine_part = jnp.sin(shift_angle)
    group_size = math.gcd(NP, 32)
    group_count = NP // group_size
    child_groups = child_of.reshape(group_count, group_size, KIDS)

    def aggregate(children):
        picked = child_field[:, :, children]
        spread = interpolate(picked, interp_index, interp_weight)
        real_part = jnp.sum(spread[0] * cosines - spread[1] * sine_part, axis=2)
        imag_part = jnp.sum(spread[0] * sine_part + spread[1] * cosines, axis=2)
        return jnp.stack([real_part, imag_part])

    outgoing = lax.map(aggregate, child_groups)
    outgoing = jnp.moveaxis(outgoing, 0, 2).reshape(2, RHS, NP, K2)

    def add_term(term, carry):
        source = jnp.take(outgoing, interaction_list[term], axis=2)
        op_real = translation[0, term]
        op_imag = translation[1, term]
        return jnp.stack([carry[0] + op_real * source[0] - op_imag * source[1],
                          carry[1] + op_real * source[1] + op_imag * source[0]])

    translated = lax.fori_loop(0, LIST, add_term, jnp.zeros_like(outgoing))

    def disaggregate(inputs):
        children, incoming = inputs
        real_part = incoming[0][:, :, None] * cosines + incoming[1][:, :, None] * sine_part
        imag_part = incoming[1][:, :, None] * cosines - incoming[0][:, :, None] * sine_part
        return anterpolate(jnp.stack([real_part, imag_part]), interp_index, interp_weight)

    grouped = jnp.moveaxis(translated.reshape(2, RHS, group_count, group_size, K2), 2, 0)
    pieces = lax.map(disaggregate, (child_groups, grouped))
    slots = jnp.moveaxis(pieces, 0, 2).reshape(2, RHS, NP * KIDS, K1)
    return jnp.zeros_like(child_field).at[:, :, child_of.reshape(-1)].set(slots)
```

```python
import jax
import jax.numpy as jnp
from jax import lax
from jax.experimental import pallas as pl
from jax.experimental.pallas import tpu as pltpu
from jax.sharding import PartitionSpec as P

F32 = jnp.float32
BF16 = jnp.bfloat16
HW = 8
KIDS = 4
PAR = 8
TERMS = 27
STENCIL = 6
EXTRA = 16
MAIN = 64
PACK_ROWS = 120
IDX_AT, WEIGHT_AT, SHIFT_AT, REAL_AT, IMAG_AT = 32, 40, 48, 56, 88


def lanes(shape=(8, 128)):
    return lax.broadcasted_iota(jnp.int32, shape, 1)


def rows(shape=(8, 128)):
    return lax.broadcasted_iota(jnp.int32, shape, 0)


def turn(value, shift):
    shift = shift % 128
    return value if shift == 0 else pltpu.roll(value, shift, 1)


def kid_rows(kids_ref, at):
    s, p = at // PAR, at % PAR
    return pl.ds(kids_ref[p * KIDS + s] % 32, 8, stride=32)


def split(value):
    high = value.astype(BF16)
    return high, (value - high.astype(F32)).astype(BF16)


def stencil_matrix(columns, weights, width, used):
    parts = []
    for group in range(used // 8):
        places = rows((8, width)) + 8 * group
        summed = jnp.zeros((8, width), F32)
        for j in range(STENCIL):
            summed = summed + jnp.where(columns[j : j + 1, :] == places, weights[j : j + 1, :], 0.0)
        parts.append(summed)
    parts.append(jnp.zeros((128 - used, width), F32))
    return split(jnp.concatenate(parts, axis=0))


def interp_product(tile, matrix):
    high, low = split(tile)
    both = jnp.concatenate([high, high], axis=1)
    return jnp.dot(both, matrix, preferred_element_type=F32) + jnp.dot(
        low, matrix[:128], preferred_element_type=F32
    )


def anterp_product(spread, matrix):
    high, low = split(spread)
    dims = (((1,), (1,)), ((), ()))
    first = lax.dot_general(high, matrix, dims, preferred_element_type=F32)
    second = lax.dot_general(low, matrix[:128], dims, preferred_element_type=F32)
    return first[:, :128] + first[:, 128:] + second


def swapped(value):
    return pltpu.roll(value, 4, 0)


def sign(width):
    return jnp.where(rows((8, width)) < 4, -1.0, 1.0).astype(F32)


def aggregate(product, cosines, sines):
    width = product.shape[1]
    flip = sign(width)
    out = []
    for p in range(PAR):
        straight = jnp.zeros((8, width), F32)
        crossed = jnp.zeros((8, width), F32)
        for s in range(KIDS):
            piece = product[(s * PAR + p) * 8 : (s * PAR + p) * 8 + 8, :]
            straight = straight + piece * cosines[s : s + 1, :]
            crossed = crossed + piece * sines[s : s + 1, :]
        out.append(straight + flip * swapped(crossed))
    return out


def send_main(out_tiles, store):
    low = lanes() < MAIN
    for q in range(PAR // 2):
        first, second = out_tiles[2 * q], out_tiles[2 * q + 1]
        store(0, q, jnp.where(low, first, turn(second, MAIN)))
        store(1, q, jnp.where(low, turn(first, MAIN), second))


def pack_kernel(kids, child_lo, child_hi, idx_lo, idx_hi, w_lo, w_hi, a_lo, a_hi, t_lo, t_hi, lo_ref, hi_ref):
    piece = lanes() // EXTRA
    for a in range(KIDS):
        low_tile = jnp.zeros((8, 128), F32)
        high_tile = jnp.zeros((8, 128), F32)
        for i in range(8):
            at = kid_rows(kids, 8 * a + i)
            low_tile = jnp.where(piece == i, turn(child_lo[at, :], 16 * i), low_tile)
            high_tile = jnp.where(piece == i, turn(child_hi[at, :], 16 * i + 16), high_tile)
        lo_ref[8 * a : 8 * a + 8, :] = low_tile
        hi_ref[8 * a : 8 * a + 8, :] = high_tile
    for ref, idx, w, a, t in ((lo_ref, idx_lo, w_lo, a_lo, t_lo), (hi_ref, idx_hi, w_hi, a_hi, t_hi)):
        ref[32:, :] = jnp.zeros((PACK_ROWS - 32, 128), F32)
        ref[IDX_AT : IDX_AT + STENCIL, :] = idx[...].astype(F32)
        ref[WEIGHT_AT : WEIGHT_AT + STENCIL, :] = w[...]
        ref[SHIFT_AT : SHIFT_AT + KIDS, :] = a[...]
        ref[REAL_AT : REAL_AT + TERMS, :] = t[0]
        ref[IMAG_AT : IMAG_AT + TERMS, :] = t[1]


def inner_kernel(kids, where, child, idx, weight, angle, send, matrices, phases, ends, raw, own, sems):
    base = where[1] * child.shape[1]
    count = child.shape[1] // 128
    copies = [
        pltpu.make_async_copy(child.at[:, 128 * t : 128 * t + 128], raw.at[t], sems.at[t])
        for t in range(count)
    ]
    for copy in copies:
        copy.start()
    for t in range(count):
        copies[t].wait()
        for at in range(PAR * KIDS):
            own[t, 8 * at : 8 * at + 8, :] = raw.at[t][kid_rows(kids, at), :]
    ends[0] = own[0]
    ends[1] = own[count - 2]
    ends[2] = own[count - 1]

    def fill_matrix(block):
        cut = pl.ds(pl.multiple_of(block * 256, 256), 256)
        high, low = stencil_matrix(
            idx[:, cut] - (base + block * 64 - HW), weight[:, cut], 256, 80
        )
        matrices[block, :128, :] = high
        matrices[block, 128:, :] = low
        cosines, sines = jnp.cos(angle[:, cut]), jnp.sin(angle[:, cut])
        phases[:KIDS, cut] = cosines
        phases[KIDS:, cut] = sines
        return cosines, sines

    wide = lanes((256, 128))

    def do_block(block, tile):
        cosines, sines = fill_matrix(block)
        out = aggregate(interp_product(tile, matrices[block]), cosines, sines)
        for u in range(2):

            def store(half, q, message):
                send[4 * block + 2 * u + half, q] = message

            send_main([o[:, 128 * u : 128 * u + 128] for o in out], store)

    def odd_tile(t):
        return jnp.where(wide < 72, pltpu.roll(own[t], 72, 1), pltpu.roll(own[t + 1], 72, 1))

    fill_matrix(0)
    fill_matrix(2 * count - 2)
    fill_matrix(2 * count - 1)
    do_block(1, odd_tile(0))

    def step(t, carry):
        even = jnp.where(wide < HW, pltpu.roll(own[t - 1], HW, 1), pltpu.roll(own[t], HW, 1))
        do_block(2 * t, even)
        do_block(2 * t + 1, odd_tile(t))
        return carry

    lax.fori_loop(1, count - 1, step, 0)


def halo_lanes(below, above, at):
    return jnp.where(lanes((at[1], 128)) < 32, turn(below[at[0] : at[0] + at[1], :], 32), turn(above[at[0] : at[0] + at[1], :], 32))


def edge_kernel(
    where, ends, below, above, matrix_lo, matrix_hi, phases_lo, phases_hi, send_in, send,
    edge_matrix, edge_phases, first, last, beyond, messages, rest, sems,
):
    base = where[1] * 1152
    lane = lanes()
    for at in range(PAR * KIDS):
        a, i = at // 8, at % 8
        cut = slice(8 * at, 8 * at + 8)
        low_halo = below[8 * a : 8 * a + 8, :]
        high_halo = above[8 * a : 8 * a + 8, :]
        low_own = ends[0, cut, :]
        high_own = ends[2, cut, :]
        first[cut, :] = jnp.where(lane < HW, turn(low_halo, -(16 * i + 8)), turn(low_own, HW))
        last[1, cut, :] = jnp.where(lane < 72, turn(high_own, 72), turn(high_halo, 72 - 16 * i))
        last[0, cut, :] = jnp.where(lane < HW, turn(ends[1, cut, :], HW), turn(high_own, HW))
        edge = jnp.where(lane < 16, turn(low_halo, -16 * i), turn(low_own, 16))
        edge = jnp.where(lane < 24, edge, turn(high_own, 32))
        beyond[cut, :] = jnp.where(lane < 32, edge, turn(high_halo, 32 - 16 * i))

    row = halo_lanes(below, above, (IDX_AT, 8)).astype(jnp.int32) - base
    row = row + jnp.where(lane < 32, 16, 24 - 1144)
    weight = jnp.where(lane < 64, halo_lanes(below, above, (WEIGHT_AT, 8)), 0.0)
    high, low = stencil_matrix(row, weight, 128, 48)
    edge_matrix[:128, :] = high
    edge_matrix[128:, :] = low
    shift = halo_lanes(below, above, (SHIFT_AT, 8))[:KIDS]
    edge_phases[:KIDS, :] = jnp.cos(shift)
    edge_phases[KIDS:, :] = jnp.sin(shift)

    out = aggregate(interp_product(first[...], matrix_lo[0]), phases_lo[:KIDS, :], phases_lo[KIDS:, :])
    for u in range(2):

        def store(half, q, message):
            messages[2 * u + half, q] = message

        send_main([o[:, 128 * u : 128 * u + 128] for o in out], store)

    tiles = []
    for k in range(2):
        cut = slice(256 * k, 256 * k + 256)
        out = aggregate(
            interp_product(last[k], matrix_hi[k]), phases_hi[:KIDS, cut], phases_hi[KIDS:, cut]
        )
        for u in range(2):
            tiles.append([o[:, 128 * u : 128 * u + 128] for o in out])
    tiles.append(
        aggregate(interp_product(beyond[...], edge_matrix[...]), edge_phases[:KIDS, :], edge_phases[KIDS:, :])
    )
    piece = lane // EXTRA
    for e in range(5):
        for i in range(8):
            message = tiles[e][0]
            message = turn(message, -16 * i)
            for p in range(1, PAR):
                message = jnp.where(piece == p, turn(tiles[e][p], 16 * (p - i)), message)
            rest[8 * e + i] = message
    rest[40:] = jnp.zeros((24, 8, 128), F32)
    one = pltpu.make_async_copy(messages, send.at[0:4, 0:4], sems.at[0])
    two = pltpu.make_async_copy(rest, send.at[:, 4], sems.at[1])
    one.start()
    two.start()
    one.wait()
    two.wait()


def translate_kernel(where, lists, received, table, table_rest, below, above, send, sources, factors):
    lane = lanes()
    box = where[0]
    low = lane < MAIN
    for c in range(2):
        at = (REAL_AT, IMAG_AT)[c]
        wide = lanes((TERMS, 128))
        main = pltpu.roll(table[c], (128 - MAIN * (box % 2)) % 128, 1)
        beyond = jnp.where(
            wide < 32,
            turn(below[at : at + TERMS, :], 32),
            turn(above[at : at + TERMS, :], 32),
        )
        extra = jnp.where(box < 32, table_rest[c], beyond)
        extra = pltpu.roll(extra, (MAIN + 128 - EXTRA * (box % 8)) % 128, 1)
        both = jnp.where(wide < MAIN, main, extra)
        for j in range(TERMS):
            factors[c, j] = jnp.broadcast_to(both[j : j + 1, :], (8, 128))

    def unpack(g, carry):
        rest = received[g, 4]
        for q in range(PAR // 2):
            message = received[g, q]
            sources[PAR * g + 2 * q] = jnp.where(low, message, turn(rest, MAIN - EXTRA * (2 * q)))
            sources[PAR * g + 2 * q + 1] = jnp.where(
                low, turn(message, MAIN), turn(rest, MAIN - EXTRA * (2 * q + 1))
            )
        return carry

    lax.fori_loop(0, received.shape[0], unpack, 0, unroll=2)
    flip = sign(128)
    piece = lane // EXTRA
    parents = sources.shape[0]

    def group(g, carry):
        straight = [jnp.zeros((8, 128), F32)] * PAR
        crossed = [jnp.zeros((8, 128), F32)] * PAR
        for j in range(TERMS):
            real, imag = factors[0, j], factors[1, j]
            for i in range(PAR):
                source = sources[lists[j * parents + g * PAR + i]]
                straight[i] = straight[i] + real * source
                crossed[i] = crossed[i] + imag * source
        out = [straight[i] + flip * swapped(crossed[i]) for i in range(PAR)]
        for q in range(PAR // 2):
            send[g, q] = jnp.where(low, out[2 * q], turn(out[2 * q + 1], MAIN))
        rest = turn(out[0], -MAIN)
        for i in range(1, PAR):
            rest = jnp.where(piece == i, turn(out[i], EXTRA * i - MAIN), rest)
        send[g, 4] = rest
        return carry

    lax.fori_loop(0, parents // PAR, group, 0)


def spread_rows(tiles, cosines, sines):
    width = tiles[0].shape[1]
    flip = -sign(width)
    crossed = [flip * swapped(tile) for tile in tiles]
    parts = []
    for s in range(KIDS):
        for p in range(PAR):
            parts.append(tiles[p] * cosines[s : s + 1, :] + crossed[p] * sines[s : s + 1, :])
    return jnp.concatenate(parts, axis=0)


def final_kernel(kids, received, matrices, phases, edge_matrix, edge_phases, out, even, odd, placed, sems):
    lane = lanes()
    low = lane < MAIN
    count = even.shape[0]

    def main_tiles(tile_at):
        tiles = [None] * PAR
        for q in range(PAR // 2):
            first, second = received[2 * tile_at, q], received[2 * tile_at + 1, q]
            tiles[2 * q] = jnp.where(low, first, turn(second, MAIN))
            tiles[2 * q + 1] = jnp.where(low, turn(first, MAIN), second)
        return tiles

    piece = lane // EXTRA

    def extra_tiles(e):
        tiles = []
        for p in range(PAR):
            tile = turn(received[8 * e, 4], -16 * p)
            for i in range(1, 8):
                tile = jnp.where(piece == i, turn(received[8 * e + i, 4], 16 * (i - p)), tile)
            tiles.append(tile)
        return tiles

    def block_of(block, tiles_at):
        left, right = tiles_at
        tiles = [jnp.concatenate([left[p], right[p]], axis=1) for p in range(PAR)]
        cut = pl.ds(block * 256, 256)
        return anterp_product(
            spread_rows(tiles, phases[:KIDS, cut], phases[KIDS:, cut]), matrices[block]
        )

    def step(t, carry):
        first = pl.multiple_of(2 * t, 2)
        even[t] = block_of(first, (main_tiles(4 * t), main_tiles(4 * t + 1)))
        odd[t] = block_of(first + 1, (main_tiles(4 * t + 2), main_tiles(4 * t + 3)))
        return carry

    lax.fori_loop(0, count - 1, step, 0)
    even[count - 1] = block_of(2 * count - 2, (extra_tiles(0), extra_tiles(1)))
    odd[count - 1] = block_of(2 * count - 1, (extra_tiles(2), extra_tiles(3)))
    tiles = [jnp.where(low, tile, 0.0) for tile in extra_tiles(4)]
    beyond = anterp_product(
        spread_rows(tiles, edge_phases[:KIDS, :], edge_phases[KIDS:, :]), edge_matrix[...]
    )

    for at in range(PAR * KIDS):
        cut = slice(8 * at, 8 * at + 8)
        place = kid_rows(kids, at)
        evens = [turn(even[t, cut, :], -HW) for t in range(count)]
        odds = [turn(odd[t, cut, :], 56) for t in range(count)]
        for t in range(count):
            from_even = jnp.where(lane < 120, evens[t], evens[t + 1] if t + 1 < count else 0.0)
            from_odd = jnp.where(lane >= HW, odds[t], odds[t - 1] if t > 0 else 0.0)
            total = from_even + from_odd
            if t == 0:
                total = total + jnp.where(lane < HW, turn(beyond[cut, :], -16), 0.0)
            if t == count - 1:
                total = total + jnp.where(lane >= 120, turn(beyond[cut, :], 96), 0.0)
            placed.at[t][place, :] = total
    copies = [
        pltpu.make_async_copy(placed.at[t], out.at[:, 128 * t : 128 * t + 128], sems.at[t])
        for t in range(count)
    ]
    for copy in copies:
        copy.start()
    for copy in copies:
        copy.wait()


def smem():
    return pl.BlockSpec(memory_space=pltpu.SMEM)


def vmem():
    return pl.BlockSpec(memory_space=pltpu.VMEM)


def any_space():
    return pl.BlockSpec(memory_space=pl.ANY)


def shards(
    child_field, child_of, shift_angle, interp_index, interp_weight, interaction_list, translation
):
    box_index = lax.axis_index("box")
    dir_index = lax.axis_index("dir")
    dirs = lax.axis_size("dir")
    boxes = lax.axis_size("box")
    halves, fields, own_boxes, strip_child = child_field.shape
    strip_par = interp_index.shape[1]
    count = strip_child // 128
    row_count = halves * fields * own_boxes
    shape = jax.ShapeDtypeStruct
    child = child_field.reshape(row_count, strip_child)
    kids = child_of.reshape(-1)
    where = jnp.stack([box_index, dir_index]).astype(jnp.int32)
    last_par = strip_par // 128 - 1

    def edge(block, at):
        index = (0,) * (len(block) - 1) + (at,)
        return pl.BlockSpec(block, lambda i, *_: index)

    both = lambda block, last: [edge(block, 0), edge(block, last)]
    lo_pack, hi_pack = pl.pallas_call(
        pack_kernel,
        grid_spec=pltpu.PrefetchScalarGridSpec(
            num_scalar_prefetch=1,
            grid=(1,),
            in_specs=both((row_count, 128), count - 1)
            + both((STENCIL, 128), last_par)
            + both((STENCIL, 128), last_par)
            + both((KIDS, 128), last_par)
            + both((2, TERMS, 128), last_par),
            out_specs=[pl.BlockSpec((PACK_ROWS, 128), lambda i, *_: (0, 0))] * 2,
        ),
        out_shape=[shape((PACK_ROWS, 128), F32)] * 2,
        name="pack",
    )(
        kids, child, child, interp_index, interp_index, interp_weight, interp_weight,
        shift_angle, shift_angle, translation, translation,
    )
    forward = [(i, i + 1) for i in range(dirs - 1)]
    backward = [(i + 1, i) for i in range(dirs - 1)]
    below = lax.ppermute(hi_pack, "dir", forward)
    above = lax.ppermute(lo_pack, "dir", backward)

    send, matrices, phases, ends = pl.pallas_call(
        inner_kernel,
        in_specs=[smem(), smem(), any_space(), vmem(), vmem(), vmem()],
        out_specs=[vmem()] * 4,
        out_shape=[
            shape((boxes, 5, 8, 128), F32),
            shape((2 * count, 256, 256), BF16),
            shape((8, strip_par), F32),
            shape((3, row_count, 128), F32),
        ],
        scratch_shapes=[pltpu.VMEM((count, row_count, 128), F32)] * 2
        + [pltpu.SemaphoreType.DMA((count,))],
        name="inner",
    )(kids, where, child, interp_index, interp_weight, shift_angle)

    def whole(*block):
        return pl.BlockSpec(block, lambda i, *_: (0,) * len(block))

    send, edge_matrix, edge_phases = pl.pallas_call(
        edge_kernel,
        grid_spec=pltpu.PrefetchScalarGridSpec(
            num_scalar_prefetch=1,
            grid=(1,),
            in_specs=[
                whole(3, row_count, 128),
                whole(PACK_ROWS, 128),
                whole(PACK_ROWS, 128),
                edge((1, 256, 256), 0),
                pl.BlockSpec((2, 256, 256), lambda i, *_: (count - 1, 0, 0)),
                edge((8, 256), 0),
                edge((8, 512), strip_par // 512 - 1),
                any_space(),
            ],
            out_specs=[any_space(), whole(256, 128), whole(8, 128)],
            scratch_shapes=[
                pltpu.VMEM((row_count, 128), F32),
                pltpu.VMEM((2, row_count, 128), F32),
                pltpu.VMEM((row_count, 128), F32),
                pltpu.VMEM((4, 4, 8, 128), F32),
                pltpu.VMEM((boxes, 8, 128), F32),
                pltpu.SemaphoreType.DMA((2,)),
            ],
        ),
        out_shape=[shape(send.shape, F32), shape((256, 128), BF16), shape((8, 128), F32)],
        input_output_aliases={8: 0},
        name="edge",
    )(where, ends, below, above, matrices, matrices, phases, phases, send)

    received = lax.all_to_all(send, "box", split_axis=0, concat_axis=0, tiled=True)
    parents = interaction_list.shape[1]
    answered = pl.pallas_call(
        translate_kernel,
        grid_spec=pltpu.PrefetchScalarGridSpec(
            num_scalar_prefetch=2,
            grid=(1,),
            in_specs=[
                pl.BlockSpec((boxes, 5, 8, 128), lambda i, *_: (0, 0, 0, 0)),
                pl.BlockSpec((2, TERMS, 128), lambda i, w, l: (0, 0, w[0] // 2)),
                pl.BlockSpec(
                    (2, TERMS, 128), lambda i, w, l: (0, 0, jnp.minimum(32 + w[0] // 8, last_par))
                ),
                pl.BlockSpec((PACK_ROWS, 128), lambda i, *_: (0, 0)),
                pl.BlockSpec((PACK_ROWS, 128), lambda i, *_: (0, 0)),
            ],
            out_specs=pl.BlockSpec((boxes, 5, 8, 128), lambda i, *_: (0, 0, 0, 0)),
            scratch_shapes=[
                pltpu.VMEM((parents, 8, 128), F32),
                pltpu.VMEM((2, TERMS, 8, 128), F32),
            ],
        ),
        out_shape=shape((boxes, 5, 8, 128), F32),
        name="translate",
    )(where, interaction_list.reshape(-1), received, translation, translation, below, above)
    incoming = lax.all_to_all(answered, "box", split_axis=0, concat_axis=0, tiled=True)

    out = pl.pallas_call(
        final_kernel,
        in_specs=[smem()] + [vmem()] * 5,
        out_specs=any_space(),
        out_shape=shape((row_count, strip_child), F32),
        scratch_shapes=[pltpu.VMEM((count, row_count, 128), F32)] * 3
        + [pltpu.SemaphoreType.DMA((count,))],
        name="final",
    )(kids, incoming, matrices, phases, edge_matrix, edge_phases)
    return out.reshape(child_field.shape)


def solution(mesh):
    in_specs = (
        P(None, None, "box", "dir"),
        P("box", None),
        P(None, "dir"),
        P(None, "dir"),
        P(None, "dir"),
        P(),
        P(None, None, "dir"),
    )
    out_specs = P(None, None, "box", "dir")
    return jax.shard_map(shards, mesh=mesh, in_specs=in_specs, out_specs=out_specs, check_vma=False)
```
